32 devices in a mesh: grp: 8 (over z, y), tp: 2 (over x), sp: 2 (over core).
Axes of the slice: x: 2, y: 2, z: 4, core: 2. Of those that a mesh axis runs over, the one named last changes fastest.
Arguments:
- tokens: bfloat16 [12288, 1536], P(('grp', 'sp')), may hold values from -6 to 6
- text_states: bfloat16 [2048, 4096], P(('grp', 'sp')), may hold values from -6 to 6
- condition: bfloat16 [8, 1024], P('grp'), may hold values from -6 to 6
- positions: int32 [3, 12288], P(None, ('grp', 'sp')), may hold values from 0 to 16, as said below
- counts: int32 [8], replicated, may hold values from 84 to 1536, as said below
- cotangent: bfloat16 [12288, 1536], P(('grp', 'sp')), may hold values from -6 to 6
- w_mod: bfloat16 [1024, 6144], P('sp', 'tp'), may hold values from -0.1875 to 0.1875
- norm_gains: float32 [4, 1536], replicated, may hold values from 0.1 to 1.9
- qk_gains: float32 [2, 1536], P(None, 'tp'), may hold values from 0.1 to 1.9
- cross_gate: float32 [24], P('tp'), may hold values from 0.25 to 1
- w_query: bfloat16 [1536, 1536], P('sp', 'tp'), may hold values from -0.15625 to 0.15625
- w_key: bfloat16 [1536, 1536], P('sp', 'tp'), may hold values from -0.15625 to 0.15625
- w_value: bfloat16 [1536, 1536], P('sp', 'tp'), may hold values from -0.15625 to 0.15625
- w_out: bfloat16 [1536, 1536], P('tp', 'sp'), may hold values from -0.15625 to 0.15625
- w_cross_query: bfloat16 [1536, 1536], P('sp', 'tp'), may hold values from -0.15625 to 0.15625
- w_cross_key: bfloat16 [4096, 1536], P('sp', 'tp'), may hold values from -0.09375 to 0.09375
- w_cross_value: bfloat16 [4096, 1536], P('sp', 'tp'), may hold values from -0.09375 to 0.09375
- w_gate: bfloat16 [1536, 4096], P('sp', 'tp'), may hold values from -0.15625 to 0.15625
- w_up: bfloat16 [1536, 4096], P('sp', 'tp'), may hold values from -0.15625 to 0.15625
- w_down: bfloat16 [4096, 1536], P('tp', 'sp'), may hold values from -0.09375 to 0.09375
Outputs:
- output: bfloat16 [12288, 1536], P(('grp', 'sp'))
- grad_tokens: float32 [12288, 1536], P(('grp', 'sp'))
- grad_text: float32 [2048, 4096], P(('grp', 'sp'), 'tp')
- grad_w_mod: float32 [1024, 6144], P(('grp', 'sp'), 'tp')
- grad_norm_gains: float32 [4, 1536], replicated
- grad_qk_gains: float32 [2, 1536], P(None, 'tp')
- grad_cross_gate: float32 [24], P('tp')
- grad_w_query: float32 [1536, 1536], P(('grp', 'sp'), 'tp')
- grad_w_key: float32 [1536, 1536], P(('grp', 'sp'), 'tp')
- grad_w_value: float32 [1536, 1536], P(('grp', 'sp'), 'tp')
- grad_w_out: float32 [1536, 1536], P('tp', ('grp', 'sp'))
- grad_w_cross_query: float32 [1536, 1536], P(('grp', 'sp'), 'tp')
- grad_w_cross_key: float32 [4096, 1536], P(('grp', 'sp'), 'tp')
- grad_w_cross_value: float32 [4096, 1536], P(('grp', 'sp'), 'tp')
- grad_w_gate: float32 [1536, 4096], P(('grp', 'sp'), 'tp')
- grad_w_up: float32 [1536, 4096], P(('grp', 'sp'), 'tp')
- grad_w_down: float32 [4096, 1536], P('tp', ('grp', 'sp'))
The draws below stay inside these ranges and needn't reach their ends.
Inputs may be any that keep to these rules, and one draw needn't show every extreme that they name: `counts`: valid tokens of each clip, at most 1536; at least one clip fills all 1536 slots. `positions`: for each clip, row 0 holds the frame, row 1 the row and row 2 the column of each valid slot: each frame is some rows of a fixed width plus one nextline column, followed by one nextframe token with the row past the last and column 0; padding slots hold zeros.
All inputs are finite; a program needn't handle non-finite values.
Results may differ from the reference program's by a relative error of at most 0.02.
Values may be sent and summed in bfloat16 or wider, within the bound.
No kernel may reach another device: no remote copies, remote signals or barrier semaphores. Data moves between devices by JAX's collectives and lax.ppermute only.
A program may use at most 448 MiB of HBM per device.

```python
import jax
import jax.numpy as jnp
from jax import lax

D = 1536
HEADS = 24
HEAD_DIM = 64
FF = 4096
COND = 1024
TXT = 4096
TXT_LEN = 256
SEQ = 1536
GROUPS = 8
TOKENS = 12288


def clip_table(key):
    folded = jax.random.fold_in(key, 4242)
    subkeys = jax.random.split(folded, 5)
    widths = jax.random.randint(subkeys[0], (GROUPS,), 4, 17)
    heights = jax.random.randint(subkeys[1], (GROUPS,), 4, 13)
    frames = jax.random.randint(subkeys[2], (GROUPS,), 4, 17)
    fullest = jax.random.randint(subkeys[3], (), 0, GROUPS)
    kept = jax.random.randint(subkeys[4], (GROUPS,), 4, 9)
    is_fullest = jnp.arange(GROUPS) == fullest
    widths = jnp.where(is_fullest, 16, widths)
    heights = jnp.where(is_fullest, 12, heights)
    period = heights * (widths + 1) + 1
    lengths = jnp.minimum(frames * period, SEQ * kept // 8)
    lengths = jnp.where(is_fullest, SEQ, lengths)
    return (widths, heights, period, lengths)


def draw_counts(key, part):
    return clip_table(key)[3].astype(jnp.int32)


def draw_positions(key, part):
    widths, heights, period, lengths = clip_table(key)
    token_index = jnp.arange(SEQ)[None, :]
    within = token_index % period[:, None]
    frame_no = token_index // period[:, None]
    row_no = within // (widths[:, None] + 1)
    column = within % (widths[:, None] + 1)
    is_last = within == period[:, None] - 1
    row_no = jnp.where(is_last, heights[:, None], row_no)
    column = jnp.where(is_last, 0, column)
    is_live = (token_index < lengths[:, None]).astype(jnp.int32)
    stacked = jnp.stack([frame_no * is_live, row_no * is_live, column * is_live])
    return stacked.reshape(3, GROUPS * SEQ).astype(jnp.int32)


def block_scale(stream_key, dims, shards, smallest, top_value):
    def one(axis_at, shards_of):
        steps = jax.random.uniform(jax.random.fold_in(jax.random.fold_in(stream_key, 6), axis_at), (shards_of,), jnp.float32, smallest / len(shards), top_value / len(shards))
        return jnp.repeat(jnp.exp(steps), dims[axis_at] // shards_of).reshape((-1,) + (1,) * (len(dims) - axis_at - 1))

    factor_of = one(*shards[0])
    for cut in shards[1:]:
        factor_of = factor_of * one(*cut)
    return factor_of


def scatter_about(own_key, extent, deviation, reach, cuts=(), held_as=jnp.bfloat16):
    array = jax.random.normal(own_key, extent, jnp.float32) * deviation
    if len(cuts) > 0:
        array = block_scale(own_key, extent, cuts, -0.22, 0.18) * array
    return jnp.clip(array, min=-reach, max=reach).astype(held_as)


def setup_inputs(seed: int = 0) -> dict:
    splits = jax.random.split(jax.random.key(seed), 21)
    tokens = scatter_about(splits[0], (TOKENS, D), 1.0, 6.0, ((0, 16),))
    text_states = scatter_about(splits[1], (GROUPS * TXT_LEN, TXT), 1.0, 6.0, ((0, 16),))
    condition = scatter_about(splits[2], (GROUPS, COND), 1.0, 6.0, ((0, 8),))
    positions = draw_positions(jax.random.fold_in(splits[20], 71), 0)
    counts = draw_counts(jax.random.fold_in(splits[20], 71), 0)
    cotangent = scatter_about(splits[5], (TOKENS, D), 1.0, 6.0, ((0, 16),))
    w_mod = scatter_about(splits[6], (COND, 4 * D), COND ** -0.5, 0.1875, ((0, 2), (1, 2)))
    norm_gains = jnp.clip(1.0 + 0.18 * jax.random.normal(splits[7], (4, D), jnp.float32), 0.1, 1.9)
    qk_gains = jnp.clip(1.0 + 0.18 * jax.random.normal(splits[8], (2, D), jnp.float32), 0.1, 1.9)
    cross_gate = jnp.clip(0.25 + 0.75 * jax.random.uniform(splits[9], (HEADS,), jnp.float32) ** block_scale(splits[9], (HEADS,), ((0, 2),), -0.2, 0.2), 0.25, 1.0)
    w_query = scatter_about(splits[10], (D, D), D ** -0.5, 0.15625, ((0, 2), (1, 2)))
    w_key = scatter_about(splits[11], (D, D), D ** -0.5, 0.15625, ((0, 2), (1, 2)))
    w_value = scatter_about(splits[12], (D, D), D ** -0.5, 0.15625, ((0, 2), (1, 2)))
    w_out = scatter_about(splits[13], (D, D), D ** -0.5, 0.15625, ((0, 2), (1, 2)))
    w_cross_query = scatter_about(splits[14], (D, D), D ** -0.5, 0.15625, ((0, 2), (1, 2)))
    w_cross_key = scatter_about(splits[15], (TXT, D), TXT ** -0.5, 0.09375, ((0, 2), (1, 2)))
    w_cross_value = scatter_about(splits[16], (TXT, D), TXT ** -0.5, 0.09375, ((0, 2), (1, 2)))
    w_gate = scatter_about(splits[17], (D, FF), D ** -0.5, 0.15625, ((0, 2), (1, 2)))
    w_up = scatter_about(splits[18], (D, FF), D ** -0.5, 0.15625, ((0, 2), (1, 2)))
    w_down = scatter_about(splits[19], (FF, D), FF ** -0.5, 0.09375, ((0, 2), (1, 2)))
    return dict(tokens=tokens, text_states=text_states, condition=condition, positions=positions, counts=counts, cotangent=cotangent, w_mod=w_mod, norm_gains=norm_gains, qk_gains=qk_gains, cross_gate=cross_gate, w_query=w_query, w_key=w_key, w_value=w_value, w_out=w_out, w_cross_query=w_cross_query, w_cross_key=w_cross_key, w_cross_value=w_cross_value, w_gate=w_gate, w_up=w_up, w_down=w_down)


@jax.custom_vjp
def low(v):
    return lax.optimization_barrier(v.astype(jnp.bfloat16)).astype(jnp.float32)

@jax.custom_vjp
def low_back(v):
    return v

def low_keep(v):
    return (low(v), None)

def low_pass(kept, grad):
    return (grad,)

def back_keep(v):
    return (v, None)

def back_low(kept, grad):
    return (low(grad),)
low.defvjp(low_keep, low_pass)
low_back.defvjp(back_keep, back_low)
EPSILON = 1e-05
ROPE_BASE = 10000.0

def matmul(left_side, right_side):
    return jnp.dot(left_side, right_side, precision=lax.Precision.HIGHEST, preferred_element_type=jnp.float32)

def normalize(values):
    return values * lax.rsqrt(lax.optimization_barrier(jnp.mean(values * values, axis=-1, keepdims=True)) + EPSILON)

def rope_angles(positions):
    pieces = []
    for axis_no, span_dims in ((0, 16), (1, 24), (2, 24)):
        frequency = ROPE_BASE ** (-2.0 * jnp.arange(span_dims // 2, dtype=jnp.float32) / span_dims)
        pieces.append(positions[axis_no].astype(jnp.float32)[:, None] * frequency[None, :])
    return jnp.concatenate(pieces, axis=1)

def rotate(values, cosine_table, sine_table):
    half_dims = values.shape[-1] // 2
    first_half = values[..., :half_dims]
    second_half = values[..., half_dims:]
    return jnp.concatenate([first_half * cosine_table - second_half * sine_table, first_half * sine_table + second_half * cosine_table], axis=-1)

def block_forward(tokens, text_states, condition, positions, valid_count, w_mod, norm_gains, qk_gains, cross_gate, w_query, w_key, w_value, w_out, w_cross_query, w_cross_key, w_cross_value, w_gate, w_up, w_down):
    length = tokens.shape[0]
    highest = lax.Precision.HIGHEST
    modulation = matmul(condition[None, :], w_mod)[0]
    scale_attn = modulation[:D]
    gate_attn = modulation[D:2 * D]
    scale_ffn = modulation[2 * D:3 * D]
    gate_ffn = modulation[3 * D:]
    scaling = HEAD_DIM ** (-0.5)
    normed_in = low(normalize(tokens) * norm_gains[0] * (1.0 + scale_attn))
    queries = normalize(low_back(matmul(normed_in, w_query)).reshape(length, HEADS, HEAD_DIM)) * qk_gains[0].reshape(HEADS, HEAD_DIM)
    key_vecs = normalize(low_back(matmul(normed_in, w_key)).reshape(length, HEADS, HEAD_DIM)) * qk_gains[1].reshape(HEADS, HEAD_DIM)
    value_vecs = low(low_back(matmul(normed_in, w_value))).reshape(length, HEADS, HEAD_DIM)
    angles = rope_angles(positions)
    cosine_table = jnp.cos(angles)[:, None, :]
    sine_table = jnp.sin(angles)[:, None, :]
    queries = low(rotate(queries, cosine_table, sine_table))
    key_vecs = low(rotate(key_vecs, cosine_table, sine_table))
    scores = low_back(jnp.einsum('qhd,khd->hqk', queries, key_vecs, precision=highest) * scaling)
    key_live = jnp.arange(length) < valid_count
    scores = jnp.where(key_live[None, None, :], scores, -1e+30)
    attn_probs = low(jax.nn.softmax(scores, axis=-1))
    self_mix = jnp.einsum('hqk,khd->qhd', attn_probs, value_vecs, precision=highest)
    cross_query = low(low_back(matmul(normed_in, w_cross_query))).reshape(length, HEADS, HEAD_DIM)
    cross_key = low(low_back(matmul(text_states, w_cross_key))).reshape(TXT_LEN, HEADS, HEAD_DIM)
    cross_value = low(low_back(matmul(text_states, w_cross_value))).reshape(TXT_LEN, HEADS, HEAD_DIM)
    cross_scores = low_back(jnp.einsum('qhd,khd->hqk', cross_query, cross_key, precision=highest) * scaling)
    cross_probs = low(jax.nn.softmax(cross_scores, axis=-1))
    cross_mix = low_back(jnp.einsum('hqk,khd->qhd', cross_probs, cross_value, precision=highest))
    mixed_heads = low(low_back(self_mix + jnp.tanh(cross_gate)[None, :, None] * cross_mix)).reshape(length, D)
    attended = low_back(matmul(mixed_heads, w_out))
    middle = tokens + jnp.tanh(gate_attn) * normalize(attended) * norm_gains[1]
    normed_mid = low(normalize(middle) * norm_gains[2] * (1.0 + scale_ffn))
    gate_pre = low_back(matmul(normed_mid, w_gate))
    up_pre = low_back(matmul(normed_mid, w_up))
    hidden = low(jax.nn.silu(gate_pre) * up_pre)
    reduced = low_back(matmul(hidden, w_down))
    return middle + jnp.tanh(gate_ffn) * normalize(reduced) * norm_gains[3]

def reference(tokens, text_states, condition, positions, counts, cotangent, w_mod, norm_gains, qk_gains, cross_gate, w_query, w_key, w_value, w_out, w_cross_query, w_cross_key, w_cross_value, w_gate, w_up, w_down):
    weights = tuple((member.astype(jnp.float32) for member in (w_mod, norm_gains, qk_gains, cross_gate, w_query, w_key, w_value, w_out, w_cross_query, w_cross_key, w_cross_value, w_gate, w_up, w_down)))
    all_valid = jnp.sum(counts).astype(jnp.float32)
    token_groups = tokens.astype(jnp.float32).reshape(GROUPS, SEQ, D)
    text_groups = text_states.astype(jnp.float32).reshape(GROUPS, TXT_LEN, TXT)
    cond_groups = condition.astype(jnp.float32)
    pos_groups = positions.reshape(3, GROUPS, SEQ).transpose(1, 0, 2)
    cot_groups = cotangent.astype(jnp.float32).reshape(GROUPS, SEQ, D)

    def one_group(running_sums, inputs):
        tok_group, text_group, cond_group, pos_group, valid_count, cot_group = inputs

        def forward(tok_in, text_in, params):
            return block_forward(tok_in, text_in, cond_group, pos_group, valid_count, *params)
        result, pullback = jax.vjp(forward, tok_group, text_group, weights)
        valid_rows = (jnp.arange(SEQ) < valid_count).astype(jnp.float32)
        grad_tok, grad_txt, grad_params = pullback(cot_group * valid_rows[:, None])
        group_share = valid_count.astype(jnp.float32) / all_valid
        running_sums = tuple((running + group_share * gradient for running, gradient in zip(running_sums, grad_params)))
        return (running_sums, (result.astype(jnp.bfloat16), grad_tok, grad_txt))
    zeros_init = tuple((jnp.zeros(member.shape, jnp.float32) for member in weights))
    summed, (outputs, grad_toks, grad_txts) = lax.scan(one_group, zeros_init, (token_groups, text_groups, cond_groups, pos_groups, counts, cot_groups))
    return (outputs.reshape(TOKENS, D), grad_toks.reshape(TOKENS, D), grad_txts.reshape(GROUPS * TXT_LEN, TXT), summed[0], summed[1], summed[2], summed[3], summed[4], summed[5], summed[6], summed[7], summed[8], summed[9], summed[10], summed[11], summed[12], summed[13])
```

```python
import jax
import jax.numpy as jnp
from jax import lax
from jax.sharding import PartitionSpec as P

HEAD_DIM = 64


EPSILON = 1e-05
ROPE_BASE = 10000.0


def rms_parts(values):
    factor = lax.rsqrt(jnp.mean(values * values, axis=-1, keepdims=True) + EPSILON)
    return (values * factor, factor)


def rms_back(gradient, normed, factor):
    return factor * (gradient - normed * jnp.mean(gradient * normed, axis=-1, keepdims=True))


def rope_angles(positions):
    pieces = []
    for axis_no, span_dims in ((0, 16), (1, 24), (2, 24)):
        frequency = ROPE_BASE ** (-2.0 * jnp.arange(span_dims // 2, dtype=jnp.float32) / span_dims)
        pieces.append(positions[axis_no].astype(jnp.float32)[:, None] * frequency[None, :])
    return jnp.concatenate(pieces, axis=1)


def rotate(values, cosine_table, sine_table):
    half_dims = values.shape[-1] // 2
    first_half = values[..., :half_dims]
    second_half = values[..., half_dims:]
    return jnp.concatenate(
        [
            first_half * cosine_table - second_half * sine_table,
            first_half * sine_table + second_half * cosine_table,
        ],
        axis=-1,
    )


def log_sum_exp(scores):
    top_score = jnp.max(scores, axis=-1, keepdims=True)
    return top_score + jnp.log(jnp.sum(jnp.exp(scores - top_score), axis=-1, keepdims=True))


def swap_sp(value):
    size = lax.axis_size("sp")
    return lax.ppermute(value, "sp", [(i, i ^ 1) for i in range(size)])


def swap_tp(value):
    size = lax.axis_size("tp")
    return lax.ppermute(value, "tp", [(i, i ^ 1) for i in range(size)])


def tp_sum(partial_sum):
    low = partial_sum.astype(jnp.bfloat16)
    return low.astype(jnp.float32) + swap_tp(low).astype(jnp.float32)


def turn_halves(values):
    half = values.shape[-1] // 2
    turned = jnp.concatenate([values[..., half:], values[..., :half]], axis=-1)
    return jnp.where(lax.axis_index("sp") == 0, values, turned)


def halve(values, axis, bit, send):
    keep_part = lax.dynamic_index_in_dim(values, bit, axis, keepdims=False)
    sent_part = lax.dynamic_index_in_dim(values, 1 - bit, axis, keepdims=False)
    return keep_part.astype(jnp.float32) + send(sent_part).astype(jnp.float32)


def weight_sum(partial_sum):
    groups = lax.axis_size("grp")
    bits = groups.bit_length() - 1
    rows = partial_sum.shape[0] // (2 * groups)
    width = partial_sum.shape[1]
    values = partial_sum.astype(jnp.bfloat16).reshape((2,) * bits + (2, rows, width))
    group_no = lax.axis_index("grp")
    summed = halve(values, bits, lax.axis_index("sp"), swap_sp)
    left = list(range(bits - 1, -1, -1))
    for exponent in [0] + list(range(bits - 1, 0, -1)):
        pairs = [(i, i ^ (1 << exponent)) for i in range(groups)]
        axis = left.index(exponent)
        left.pop(axis)
        bit = (group_no >> exponent) & 1
        summed = halve(
            summed.astype(jnp.bfloat16), axis, bit, lambda sent: lax.ppermute(sent, "grp", pairs)
        )
    return summed


def pair_plan(
    tokens,
    text_states,
    condition,
    positions,
    counts,
    cotangent,
    w_mod,
    norm_gains,
    qk_gains,
    cross_gate,
    w_query,
    w_key,
    w_value,
    w_out,
    w_cross_query,
    w_cross_key,
    w_cross_value,
    w_gate,
    w_up,
    w_down,
):
    sp_index = lax.axis_index("sp")
    own_front = jnp.concatenate([w_query, w_key, w_value, w_cross_query], axis=1)
    own_text = jnp.concatenate([w_cross_key, w_cross_value], axis=1)
    w_front = jnp.concatenate([own_front, swap_sp(own_front)], axis=0)
    w_text = jnp.concatenate([own_text, swap_sp(own_text)], axis=0)
    w_out = lax.all_gather(w_out, "sp", axis=1, tiled=True)
    w_gate = lax.all_gather(w_gate, "sp", axis=0, tiled=True)
    w_up = lax.all_gather(w_up, "sp", axis=0, tiled=True)
    w_down = lax.all_gather(w_down, "sp", axis=1, tiled=True)
    rows_here = tokens.shape[0]
    model_width = tokens.shape[1]
    local_width = w_query.shape[1]
    text_width = text_states.shape[1]
    heads_here = local_width // HEAD_DIM
    text_rows = text_states.shape[0]
    sequence_len = rows_here * lax.axis_size("sp")
    scaling = HEAD_DIM ** (-0.5)
    group_no = lax.axis_index("grp")
    valid_count = jnp.sum(jnp.where(jnp.arange(counts.shape[0]) == group_no, counts, 0))
    group_share = valid_count.astype(jnp.float32) / jnp.sum(counts).astype(jnp.float32)
    row_ids = lax.axis_index("sp") * rows_here + jnp.arange(rows_here)
    valid_rows = (row_ids < valid_count).astype(jnp.float32)[:, None]
    other_ids = (1 - sp_index) * rows_here + jnp.arange(rows_here)
    key_live = (jnp.concatenate([row_ids, other_ids]) < valid_count)[None, None, :]
    condition_rows = w_mod.shape[0]
    own_condition = lax.dynamic_slice_in_dim(
        condition, sp_index * condition_rows, condition_rows, axis=1
    )
    part_mod = jnp.dot(own_condition, w_mod, preferred_element_type=jnp.float32)
    part_mod = part_mod + swap_sp(part_mod)
    other_mod = swap_tp(part_mod)
    tp_first = lax.axis_index("tp") == 0
    modulation = jnp.concatenate(
        [jnp.where(tp_first, part_mod, other_mod), jnp.where(tp_first, other_mod, part_mod)],
        axis=1,
    )[0]
    scale_attn = modulation[:model_width]
    gate_attn = modulation[model_width : 2 * model_width]
    scale_ffn = modulation[2 * model_width : 3 * model_width]
    gate_ffn = modulation[3 * model_width :]
    tokens_wide = tokens.astype(jnp.float32)
    normed_one, factor_one = rms_parts(tokens_wide)
    lift_attn = norm_gains[0] * (1.0 + scale_attn)
    normed_in = (normed_one * lift_attn).astype(jnp.bfloat16)
    front = jnp.dot(turn_halves(normed_in), w_front, preferred_element_type=jnp.float32)
    query_pre = front[:, :local_width].reshape(rows_here, heads_here, HEAD_DIM)
    key_pre = front[:, local_width : 2 * local_width].reshape(rows_here, heads_here, HEAD_DIM)
    value_low = front[:, 2 * local_width : 3 * local_width].astype(jnp.bfloat16)
    query_gain = qk_gains[0].reshape(heads_here, HEAD_DIM)
    key_gain = qk_gains[1].reshape(heads_here, HEAD_DIM)
    query_norm, query_factor = rms_parts(query_pre)
    key_norm, key_factor = rms_parts(key_pre)
    angles = rope_angles(positions)
    cosine_table = jnp.cos(angles)[:, None, :]
    sine_table = jnp.sin(angles)[:, None, :]
    query_rot = rotate(query_norm * query_gain, cosine_table, sine_table).astype(jnp.bfloat16)
    key_rot = rotate(key_norm * key_gain, cosine_table, sine_table).astype(jnp.bfloat16)
    own_pair = jnp.concatenate([key_rot.reshape(rows_here, local_width), value_low], axis=1)
    all_pair = jnp.concatenate([own_pair, swap_sp(own_pair)], axis=0)
    key_all = all_pair[:, :local_width]
    value_all = all_pair[:, local_width:]
    key_all = key_all.reshape(sequence_len, heads_here, HEAD_DIM)
    value_all = value_all.reshape(sequence_len, heads_here, HEAD_DIM)

    def self_scores():
        raw_scores = (
            jnp.einsum("qhd,khd->hqk", query_rot, key_all, preferred_element_type=jnp.float32)
            * scaling
        )
        return jnp.where(key_live, raw_scores, -1e30)

    scores = self_scores()
    self_lse = log_sum_exp(scores)
    self_probs = jnp.exp(scores - self_lse).astype(jnp.bfloat16)
    self_mix = jnp.einsum("hqk,khd->qhd", self_probs, value_all, preferred_element_type=jnp.float32)
    cross_query = (
        front[:, 3 * local_width :].astype(jnp.bfloat16).reshape(rows_here, heads_here, HEAD_DIM)
    )
    own_cross = jnp.dot(
        turn_halves(text_states), w_text, preferred_element_type=jnp.float32
    ).astype(jnp.bfloat16)
    all_cross = jnp.concatenate([own_cross, swap_sp(own_cross)], axis=0)
    cross_keys = all_cross[:, :local_width]
    cross_values = all_cross[:, local_width:]
    text_len = cross_keys.shape[0]
    cross_keys = cross_keys.reshape(text_len, heads_here, HEAD_DIM)
    cross_values = cross_values.reshape(text_len, heads_here, HEAD_DIM)

    def cross_scores_of():
        return (
            jnp.einsum("qhd,khd->hqk", cross_query, cross_keys, preferred_element_type=jnp.float32)
            * scaling
        )

    cross_scores = cross_scores_of()
    cross_lse = log_sum_exp(cross_scores)
    cross_probs = jnp.exp(cross_scores - cross_lse).astype(jnp.bfloat16)
    cross_mix = jnp.einsum(
        "hqk,khd->qhd", cross_probs, cross_values, preferred_element_type=jnp.float32
    )
    gate_tanh = jnp.tanh(cross_gate)[None, :, None]
    mixed_heads = (
        (self_mix + gate_tanh * cross_mix).reshape(rows_here, local_width).astype(jnp.bfloat16)
    )
    attended = tp_sum(jnp.dot(mixed_heads, w_out, preferred_element_type=jnp.float32))
    attn_norm, attn_factor = rms_parts(attended)
    tanh_attn = jnp.tanh(gate_attn)
    middle = tokens_wide + tanh_attn * attn_norm * norm_gains[1]
    normed_two, factor_two = rms_parts(middle)
    lift_ffn = norm_gains[2] * (1.0 + scale_ffn)
    normed_mid = (normed_two * lift_ffn).astype(jnp.bfloat16)
    gate_pre = jnp.dot(normed_mid, w_gate, preferred_element_type=jnp.float32)
    up_pre = jnp.dot(normed_mid, w_up, preferred_element_type=jnp.float32)
    sigmoid_gate = jax.nn.sigmoid(gate_pre)
    silu_gate = gate_pre * sigmoid_gate
    hidden = (silu_gate * up_pre).astype(jnp.bfloat16)
    reduced = tp_sum(jnp.dot(hidden, w_down, preferred_element_type=jnp.float32))
    down_norm, down_factor = rms_parts(reduced)
    tanh_ffn = jnp.tanh(gate_ffn)
    output = (middle + tanh_ffn * down_norm * norm_gains[3]).astype(jnp.bfloat16)
    grad_out = cotangent.astype(jnp.float32) * valid_rows
    grad_gate_ffn = jnp.sum(grad_out * down_norm * norm_gains[3], axis=0) * (
        1.0 - tanh_ffn * tanh_ffn
    )
    grad_gain_four = jnp.sum(grad_out * tanh_ffn * down_norm, axis=0)
    grad_reduced = rms_back(grad_out * tanh_ffn * norm_gains[3], down_norm, down_factor).astype(
        jnp.bfloat16
    )
    grad_w_down = weight_sum(
        group_share
        * jnp.einsum("td,tf->df", grad_reduced, hidden, preferred_element_type=jnp.float32)
    ).T
    grad_hidden = jnp.einsum("td,fd->tf", grad_reduced, w_down, preferred_element_type=jnp.float32)
    grad_up = (grad_hidden * silu_gate).astype(jnp.bfloat16)
    grad_gate_pre = (
        grad_hidden * up_pre * sigmoid_gate * (1.0 + gate_pre * (1.0 - sigmoid_gate))
    ).astype(jnp.bfloat16)
    grad_w_gate = weight_sum(
        group_share
        * jnp.einsum("tc,tf->cf", normed_mid, grad_gate_pre, preferred_element_type=jnp.float32)
    )
    grad_w_up = weight_sum(
        group_share
        * jnp.einsum("tc,tf->cf", normed_mid, grad_up, preferred_element_type=jnp.float32)
    )
    grad_normed_mid = tp_sum(
        jnp.einsum("tf,cf->tc", grad_gate_pre, w_gate, preferred_element_type=jnp.float32)
        + jnp.einsum("tf,cf->tc", grad_up, w_up, preferred_element_type=jnp.float32)
    )
    grad_gain_three = jnp.sum(grad_normed_mid * normed_two * (1.0 + scale_ffn), axis=0)
    grad_scale_ffn = jnp.sum(grad_normed_mid * normed_two * norm_gains[2], axis=0)
    grad_middle = grad_out + rms_back(grad_normed_mid * lift_ffn, normed_two, factor_two)
    grad_gate_attn = jnp.sum(grad_middle * attn_norm * norm_gains[1], axis=0) * (
        1.0 - tanh_attn * tanh_attn
    )
    grad_gain_two = jnp.sum(grad_middle * tanh_attn * attn_norm, axis=0)
    grad_attended = rms_back(
        grad_middle * tanh_attn * norm_gains[1], attn_norm, attn_factor
    ).astype(jnp.bfloat16)
    grad_w_out = weight_sum(
        group_share
        * jnp.einsum("td,th->dh", grad_attended, mixed_heads, preferred_element_type=jnp.float32)
    ).T
    grad_mixed = (
        jnp.einsum("td,hd->th", grad_attended, w_out, preferred_element_type=jnp.float32)
        .astype(jnp.bfloat16)
        .reshape(rows_here, heads_here, HEAD_DIM)
    )
    grad_mixed_wide = grad_mixed.astype(jnp.float32)
    tanh_cross = jnp.tanh(cross_gate)
    grad_cross_gate = jnp.sum(grad_mixed_wide * cross_mix, axis=(0, 2)) * (
        1.0 - tanh_cross * tanh_cross
    )
    grad_cross_mix = (gate_tanh * grad_mixed_wide).astype(jnp.bfloat16)
    scores = self_scores()
    probs_wide = jnp.exp(scores - self_lse)
    probs_low = probs_wide.astype(jnp.bfloat16)
    grad_probs = jnp.einsum(
        "qhd,khd->hqk", grad_mixed, value_all, preferred_element_type=jnp.float32
    )
    grad_scores = (
        probs_wide * (grad_probs - jnp.sum(probs_wide * grad_probs, axis=-1, keepdims=True))
    ).astype(jnp.bfloat16)
    grad_query_rot = (
        jnp.einsum("hqk,khd->qhd", grad_scores, key_all, preferred_element_type=jnp.float32)
        * scaling
    )
    score_rows = grad_scores
    prob_rows = probs_low
    grad_key_rows = (
        jnp.einsum("hqk,qhd->khd", score_rows, query_rot, preferred_element_type=jnp.float32)
        * scaling
    )
    grad_value_rows = jnp.einsum(
        "hqk,qhd->khd", prob_rows, grad_mixed, preferred_element_type=jnp.float32
    )
    partial_pair = jnp.concatenate(
        [
            grad_key_rows.reshape(2 * rows_here, local_width),
            grad_value_rows.reshape(2 * rows_here, local_width),
        ],
        axis=1,
    ).astype(jnp.bfloat16)
    key_grads = partial_pair[:rows_here].astype(jnp.float32) + swap_sp(
        partial_pair[rows_here:]
    ).astype(jnp.float32)
    grad_key_rot = key_grads[:, :local_width].reshape(rows_here, heads_here, HEAD_DIM)
    grad_value = key_grads[:, local_width:].astype(jnp.bfloat16)
    grad_query_gained = rotate(grad_query_rot, cosine_table, -sine_table)
    grad_key_gained = rotate(grad_key_rot, cosine_table, -sine_table)
    grad_query_gain = jnp.sum(grad_query_gained * query_norm, axis=0)
    grad_key_gain = jnp.sum(grad_key_gained * key_norm, axis=0)
    grad_query = (
        rms_back(grad_query_gained * query_gain, query_norm, query_factor)
        .reshape(rows_here, local_width)
        .astype(jnp.bfloat16)
    )
    grad_key = (
        rms_back(grad_key_gained * key_gain, key_norm, key_factor)
        .reshape(rows_here, local_width)
        .astype(jnp.bfloat16)
    )
    cross_scores = cross_scores_of()
    cross_wide = jnp.exp(cross_scores - cross_lse)
    cross_low = cross_wide.astype(jnp.bfloat16)
    grad_cross_probs = jnp.einsum(
        "qhd,khd->hqk", grad_cross_mix, cross_values, preferred_element_type=jnp.float32
    )
    grad_cross_scores = (
        cross_wide
        * (grad_cross_probs - jnp.sum(cross_wide * grad_cross_probs, axis=-1, keepdims=True))
    ).astype(jnp.bfloat16)
    grad_cross_query = (
        (
            jnp.einsum(
                "hqk,khd->qhd", grad_cross_scores, cross_keys, preferred_element_type=jnp.float32
            )
            * scaling
        )
        .reshape(rows_here, local_width)
        .astype(jnp.bfloat16)
    )
    score_rows = grad_cross_scores
    prob_rows = cross_low
    grad_key_rows = (
        jnp.einsum("hqk,qhd->khd", score_rows, cross_query, preferred_element_type=jnp.float32)
        * scaling
    )
    grad_value_rows = jnp.einsum(
        "hqk,qhd->khd", prob_rows, grad_cross_mix, preferred_element_type=jnp.float32
    )
    partial_pair = jnp.concatenate(
        [
            grad_key_rows.reshape(2 * text_rows, local_width),
            grad_value_rows.reshape(2 * text_rows, local_width),
        ],
        axis=1,
    ).astype(jnp.bfloat16)
    text_grads_local = partial_pair[:text_rows].astype(jnp.float32) + swap_sp(
        partial_pair[text_rows:]
    ).astype(jnp.float32)
    text_grads = text_grads_local.astype(jnp.bfloat16)
    grad_w_text = weight_sum(
        group_share
        * jnp.einsum("tc,tf->cf", text_states, text_grads, preferred_element_type=jnp.float32)
    )
    text_partial = turn_halves(
        jnp.einsum("tf,cf->tc", text_grads, w_text, preferred_element_type=jnp.float32)
    ).astype(jnp.bfloat16)
    text_half = text_width // 2
    text_pieces = text_partial.reshape(text_rows, 2, text_half)
    grad_text = halve(text_pieces, 1, lax.axis_index("tp"), swap_tp)
    front_grads = jnp.concatenate([grad_query, grad_key, grad_value, grad_cross_query], axis=1)
    grad_w_front = weight_sum(
        group_share
        * jnp.einsum("tc,tf->cf", normed_in, front_grads, preferred_element_type=jnp.float32)
    )
    input_partial = turn_halves(
        jnp.einsum("tf,cf->tc", front_grads, w_front, preferred_element_type=jnp.float32)
    )
    grad_normed_in = tp_sum(input_partial)
    grad_gain_one = jnp.sum(grad_normed_in * normed_one * (1.0 + scale_attn), axis=0)
    grad_scale_attn = jnp.sum(grad_normed_in * normed_one * norm_gains[0], axis=0)
    grad_tokens = grad_middle + rms_back(grad_normed_in * lift_attn, normed_one, factor_one)
    grad_modulation = jnp.concatenate(
        [grad_scale_attn, grad_gate_attn, grad_scale_ffn, grad_gate_ffn]
    )
    mod_width = w_mod.shape[1]
    own_modulation = lax.dynamic_slice_in_dim(
        grad_modulation, lax.axis_index("tp") * mod_width, mod_width
    )
    small = jnp.concatenate(
        [
            own_modulation,
            group_share * jnp.concatenate([grad_gain_one, grad_gain_two]),
            group_share * jnp.concatenate([grad_gain_three, grad_gain_four]),
            group_share * jnp.concatenate([grad_query_gain.reshape(-1), grad_key_gain.reshape(-1)]),
            group_share * grad_cross_gate,
        ]
    )
    small_len = small.shape[0]
    small = jnp.pad(small, (0, -small_len % 1024)).reshape(-1, 128)
    small_all = lax.all_gather(small, ("grp", "sp"), axis=0).reshape(
        2 * counts.shape[0], small.shape[0] * 128
    )
    mod_all = jnp.sum(small_all[:, :mod_width].reshape(-1, 2, mod_width), axis=1)
    gain_sums = jnp.sum(small_all[:, mod_width:small_len], axis=0)
    gains_end = 4 * model_width
    qk_end = gains_end + 2 * local_width
    shares = counts.astype(jnp.float32) / jnp.sum(counts).astype(jnp.float32)
    block_rows = condition.shape[1] // (2 * counts.shape[0])
    block_no = 2 * group_no + sp_index
    condition_all = lax.all_gather(condition, "grp", axis=0, tiled=True)
    block_condition = lax.dynamic_slice_in_dim(
        condition_all, block_no * block_rows, block_rows, axis=1
    ).astype(jnp.float32)
    grad_w_mod = jnp.einsum(
        "gc,gf->cf", block_condition, shares[:, None] * mod_all, precision=lax.Precision.HIGHEST
    )
    return (
        output,
        grad_tokens,
        grad_text,
        grad_w_mod,
        gain_sums[:gains_end].reshape(4, model_width),
        gain_sums[gains_end:qk_end].reshape(2, local_width),
        gain_sums[qk_end:],
        grad_w_front[:, :local_width],
        grad_w_front[:, local_width : 2 * local_width],
        grad_w_front[:, 2 * local_width : 3 * local_width],
        grad_w_out,
        grad_w_front[:, 3 * local_width :],
        grad_w_text[:, :local_width],
        grad_w_text[:, local_width:],
        grad_w_gate,
        grad_w_up,
        grad_w_down,
    )


def on_device(
    tokens,
    text_states,
    condition,
    positions,
    counts,
    cotangent,
    w_mod,
    norm_gains,
    qk_gains,
    cross_gate,
    w_query,
    w_key,
    w_value,
    w_out,
    w_cross_query,
    w_cross_key,
    w_cross_value,
    w_gate,
    w_up,
    w_down,
):
    results = pair_plan(
        tokens,
        text_states,
        condition,
        positions,
        counts,
        cotangent,
        w_mod,
        norm_gains,
        qk_gains,
        cross_gate,
        w_query,
        w_key,
        w_value,
        w_out,
        w_cross_query,
        w_cross_key,
        w_cross_value,
        w_gate,
        w_up,
        w_down,
    )
    return results


def solution(mesh):
    placed = (
        P(("grp", "sp"), None),
        P(("grp", "sp"), None),
        P("grp", None),
        P(None, ("grp", "sp")),
        P(),
        P(("grp", "sp"), None),
        P("sp", "tp"),
        P(),
        P(None, "tp"),
        P("tp"),
        P("sp", "tp"),
        P("sp", "tp"),
        P("sp", "tp"),
        P("tp", "sp"),
        P("sp", "tp"),
        P("sp", "tp"),
        P("sp", "tp"),
        P("sp", "tp"),
        P("sp", "tp"),
        P("tp", "sp"),
    )
    return jax.shard_map(
        on_device,
        mesh=mesh,
        in_specs=placed,
        out_specs=(
            P(("grp", "sp"), None),
            P(("grp", "sp"), None),
            P(("grp", "sp"), "tp"),
            P(("grp", "sp"), "tp"),
            P(),
            P(None, "tp"),
            P("tp"),
            P(("grp", "sp"), "tp"),
            P(("grp", "sp"), "tp"),
            P(("grp", "sp"), "tp"),
            P("tp", ("grp", "sp")),
            P(("grp", "sp"), "tp"),
            P(("grp", "sp"), "tp"),
            P(("grp", "sp"), "tp"),
            P(("grp", "sp"), "tp"),
            P(("grp", "sp"), "tp"),
            P("tp", ("grp", "sp")),
        ),
        check_vma=False,
    )
```
